32 devices in a mesh: section: 4 (over x, core), dp: 2 (over y), ctx: 4 (over z).
Axes of the slice: x: 2, y: 2, z: 4, core: 2. Of those that a mesh axis runs over, the one named last changes fastest.
Arguments:
- layer_input: bfloat16 [4, 2, 512, 4096], P('section', 'dp', 'ctx'), may hold values from -6 to 6
- attn_grad: bfloat16 [4, 2, 512, 4096], P('section', 'dp', 'ctx'), may hold values from -48 to 48
- queries: bfloat16 [4, 2, 512, 4096], P('section', 'dp', None, 'ctx'), may hold values from -6 to 6
- keys: bfloat16 [4, 2, 512, 512], P('section', 'dp', 'ctx'), may hold values from -6 to 6
- values: bfloat16 [4, 2, 512, 512], P('section', 'dp', 'ctx'), may hold values from -4 to 4
- kv_weight: bfloat16 [4, 4096, 1024], P('section', 'ctx'), may hold values from -0.09375 to 0.09375
- segments: int32 [2, 512], P('dp'), may hold values from 0 to 3, as said below
- positions: int32 [2, 512], P('dp'), may hold values from 0 to 16383, as said below
Outputs:
- grad_prev: bfloat16 [4, 2, 512, 4096], P('section', 'dp', 'ctx')
- query_grad: bfloat16 [4, 2, 512, 4096], P('section', 'dp', 'ctx')
- weight_grad: float32 [4, 4096, 1024], P('section', 'ctx', 'dp')
The draws below stay inside these ranges and needn't reach their ends.
Inputs may be any that keep to these rules, and one draw needn't show every extreme that they name: `segments`: every sequence holds four documents: segment ids start at 0, never fall, and end at 3. Inside a segment positions rise by one a token.
All inputs are finite; a program needn't handle non-finite values.
Results may differ from the reference program's by a relative error of at most 0.012.
Values may be sent and summed in bfloat16 or wider, within the bound.
No kernel may reach another device: no remote copies, remote signals or barrier semaphores. Data moves between devices by JAX's collectives and lax.ppermute only.
A program may use at most 128 MiB of HBM per device.

```python
import math
import jax
import jax.numpy as jnp
import numpy as np
from jax import lax

D = 4096
QUERY_HEADS = 32
KEY_VALUE_HEADS = 4
HEAD_WIDTH = 128
POSMAX = 16384
LAYER_SECTIONS = 4
BATCH_COUNT = 2
SEQUENCE_TOKENS = 512
KVW = 512


def query_key_pair(key):
    key_q, key_k = jax.random.split(jax.random.fold_in(key, 11), 2)
    query_layout = (LAYER_SECTIONS, BATCH_COUNT, SEQUENCE_TOKENS, QUERY_HEADS * HEAD_WIDTH)
    key_shape = (LAYER_SECTIONS, BATCH_COUNT, SEQUENCE_TOKENS, KVW)
    query_vals = jnp.clip(jax.random.normal(key_q, query_layout, jnp.float32), -4.0, 4.0)
    key_vals = jnp.clip(jax.random.normal(key_k, key_shape, jnp.float32), -4.0, 4.0)
    return (query_vals, key_vals)


def draw_queries(key, part):
    return query_key_pair(key)[0].astype(jnp.bfloat16)


def draw_keys(key, part):
    return query_key_pair(key)[1].astype(jnp.bfloat16)


def doc_layout(key):
    key_start, key_offset = jax.random.split(jax.random.fold_in(key, 23))
    row_keys = jax.random.split(key_start, BATCH_COUNT)

    def one_row(row_key):
        chosen = jax.random.permutation(row_key, SEQUENCE_TOKENS - 1)[:3] + 1
        marks = jnp.zeros((SEQUENCE_TOKENS,), jnp.int32).at[chosen].set(1)
        return marks.at[0].set(1)
    starts = jax.vmap(one_row)(row_keys) > 0
    seg_ids = jnp.cumsum(starts.astype(jnp.int32), axis=1) - 1
    token_ids = jnp.broadcast_to(jnp.arange(SEQUENCE_TOKENS, dtype=jnp.int32)[None, :], (BATCH_COUNT, SEQUENCE_TOKENS))
    begins = lax.cummax(jnp.where(starts, token_ids, 0), axis=1)
    offsets = jax.random.randint(key_offset, (BATCH_COUNT, SEQUENCE_TOKENS), 0, POSMAX - SEQUENCE_TOKENS + 1)
    doc_offset = jnp.take_along_axis(offsets, seg_ids, axis=1)
    return (seg_ids, doc_offset + token_ids - begins)


def draw_segments(key, part):
    return doc_layout(key)[0].astype(jnp.int32)


def draw_positions(key, part):
    return doc_layout(key)[1].astype(jnp.int32)


def steps_of(rng, extent, cuts, smallest, largest):
    def one(axis_at, blocks):
        heights = jax.random.uniform(jax.random.fold_in(jax.random.fold_in(rng, 6), axis_at), (blocks,), jnp.float32, smallest / len(cuts), largest / len(cuts))
        return jnp.repeat(jnp.exp(heights), extent[axis_at] // blocks).reshape((-1,) + (1,) * (len(extent) - axis_at - 1))

    level = one(*cuts[0])
    for cut in cuts[1:]:
        level = level * one(*cut)
    return level


def scatter_about(own_key, shape, spread, reach, shards=(), kind=jnp.bfloat16):
    array = spread * jax.random.normal(own_key, shape, jnp.float32)
    if shards:
        array = array * steps_of(own_key, shape, shards, -0.22, 0.18)
    return jnp.clip(array, -reach, reach).astype(kind)


def setup_inputs(seed: int = 0) -> dict:
    streams_of = jax.random.split(jax.random.key(seed), 9)
    layer_input = scatter_about(streams_of[0], (LAYER_SECTIONS, BATCH_COUNT, SEQUENCE_TOKENS, D), 1.0, 6.0, ((0, 4), (1, 2), (2, 4)))
    attn_grad = scatter_about(streams_of[1], (LAYER_SECTIONS, BATCH_COUNT, SEQUENCE_TOKENS, QUERY_HEADS * HEAD_WIDTH), 8.0, 48.0, ((0, 4), (1, 2), (2, 4)))
    queries = draw_queries(jax.random.fold_in(streams_of[8], 71), 0)
    keys = draw_keys(jax.random.fold_in(streams_of[8], 71), 0)
    values = scatter_about(streams_of[4], (LAYER_SECTIONS, BATCH_COUNT, SEQUENCE_TOKENS, KVW), 1.0, 4.0, ((0, 4), (1, 2), (2, 4)))
    kv_weight = scatter_about(streams_of[5], (LAYER_SECTIONS, D, 2 * KVW), D ** -0.5, 0.09375, ((0, 4), (1, 4)))
    segments = draw_segments(jax.random.fold_in(streams_of[8], 71), 0)
    positions = draw_positions(jax.random.fold_in(streams_of[8], 71), 0)
    return {"layer_input": layer_input, "attn_grad": attn_grad, "queries": queries, "keys": keys, "values": values, "kv_weight": kv_weight, "segments": segments, "positions": positions}


def yarn_table(head_size):
    theta_base = 1000000.0
    factor = 4.0
    pretrain_len = 32768.0
    exponent = np.arange(0, head_size, 2) / head_size
    extrapolated = 1.0 / (theta_base ** exponent)
    interpolated = extrapolated / factor

    def boundary(rotations):
        return head_size * math.log(pretrain_len / (rotations * 2.0 * math.pi)) / (2.0 * math.log(theta_base))

    lower_dim = max(math.floor(boundary(32.0)), 0)
    upper_dim = min(math.ceil(boundary(1.0)), head_size - 1)
    ramp_width = max(upper_dim - lower_dim, 0.001)
    ramp_share = np.clip((np.arange(head_size // 2) - lower_dim) / ramp_width, 0.0, 1.0)
    keep_share = 1.0 - ramp_share
    frequency = interpolated * (1.0 - keep_share) + extrapolated * keep_share
    return frequency.astype(np.float32), float(0.1 * math.log(factor) + 1.0)


def rotate_back(gradient, places, frequency, mscale):
    angles = places.astype(jnp.float32)[:, None] * frequency[None, :]
    cosine = jnp.cos(angles) * mscale
    sine_term = jnp.sin(angles) * mscale
    cosine = jnp.concatenate([cosine, cosine], -1)[:, None, :]
    sine_term = jnp.concatenate([sine_term, sine_term], -1)[:, None, :]
    half_size = gradient.shape[-1] // 2
    turned = jnp.concatenate([gradient[..., half_size:], -gradient[..., :half_size]], -1)
    return gradient * cosine + turned * sine_term


def bf16_round(values_in):
    return lax.optimization_barrier(values_in.astype(jnp.bfloat16)).astype(jnp.float32)


def attend_item(query_row_block, key_row_block, value_row_block, output_gradient, seg_ids):
    sequence_length = query_row_block.shape[0]
    group_share_count = QUERY_HEADS // KEY_VALUE_HEADS
    score_scale = HEAD_WIDTH ** -0.5
    query_complete = query_row_block.astype(jnp.float32).reshape(sequence_length, KEY_VALUE_HEADS, group_share_count, HEAD_WIDTH)
    key_complete = key_row_block.astype(jnp.float32).reshape(sequence_length, KEY_VALUE_HEADS, HEAD_WIDTH)
    value_complete = value_row_block.astype(jnp.float32).reshape(sequence_length, KEY_VALUE_HEADS, HEAD_WIDTH)
    gradient_total = output_gradient.astype(jnp.float32).reshape(sequence_length, KEY_VALUE_HEADS, group_share_count, HEAD_WIDTH)
    block_rows = min(512, sequence_length)
    dq_parts = []
    key_gradient = jnp.zeros((sequence_length, KEY_VALUE_HEADS, HEAD_WIDTH), jnp.float32)
    value_gradient = jnp.zeros((sequence_length, KEY_VALUE_HEADS, HEAD_WIDTH), jnp.float32)
    for block_index in range(sequence_length // block_rows):
        row_start = block_index * block_rows
        row_stop = row_start + block_rows
        q_blk = query_complete[row_start:row_stop]
        k_blk = key_complete[:row_stop]
        v_blk = value_complete[:row_stop]
        g_blk = gradient_total[row_start:row_stop]
        scores = jnp.einsum('qkgd,lkd->kgql', q_blk, k_blk) * score_scale
        row_ids = jnp.arange(row_start, row_stop)[:, None]
        col_ids = jnp.arange(row_stop)[None, :]
        allowed = (col_ids <= row_ids) & (seg_ids[row_start:row_stop][:, None] == seg_ids[:row_stop][None, :])
        scores = jnp.where(allowed, scores, -1e30)
        row_max = jnp.max(scores, -1, keepdims=True)
        shifted = jnp.exp(scores - row_max)
        row_total = jnp.sum(shifted, -1, keepdims=True)
        attention = shifted / row_total
        probs_half = bf16_round(attention)
        outputs = jnp.einsum('kgql,lkd->qkgd', probs_half, v_blk)
        row_delta = jnp.transpose(jnp.sum(g_blk * outputs, -1), (1, 2, 0))[..., None]
        dprobs = jnp.einsum('qkgd,lkd->kgql', g_blk, v_blk)
        dscore_half = bf16_round(attention * (dprobs - row_delta))
        dq_parts.append(jnp.einsum('kgql,lkd->qkgd', dscore_half, k_blk) * score_scale)
        key_gradient = key_gradient.at[:row_stop].add(jnp.einsum('kgql,qkgd->lkd', dscore_half, q_blk) * score_scale)
        value_gradient = value_gradient.at[:row_stop].add(jnp.einsum('kgql,qkgd->lkd', probs_half, g_blk))
    query_grad = jnp.concatenate(dq_parts, 0).reshape(sequence_length, QUERY_HEADS, HEAD_WIDTH)
    return query_grad, key_gradient, value_gradient


def reference(layer_input, attn_grad, queries, keys, values, kv_weight, segments, positions):
    frequency, mscale = yarn_table(HEAD_WIDTH)

    def per_section(section_args):
        inputs_s, grad_s, query_s, key_s, value_s, weight = section_args

        def per_sequence(seq_args):
            inputs, output_gradient, query_row_block, key_row_block, value_row_block, seg_ids, places = seq_args
            query_grad, key_gradient, value_gradient = attend_item(query_row_block, key_row_block, value_row_block, output_gradient, seg_ids)
            query_out = rotate_back(query_grad, places, frequency, mscale).astype(jnp.bfloat16).reshape(SEQUENCE_TOKENS, QUERY_HEADS * HEAD_WIDTH)
            key_back = rotate_back(key_gradient, places, frequency, mscale).reshape(SEQUENCE_TOKENS, KVW)
            kv_grad = jnp.concatenate([key_back, value_gradient.reshape(SEQUENCE_TOKENS, KVW)], 1).astype(jnp.bfloat16)
            back_rows = jnp.dot(kv_grad, weight.T, preferred_element_type=jnp.float32).astype(jnp.bfloat16)
            weight_part = jnp.dot(inputs.T, kv_grad, preferred_element_type=jnp.float32)
            return back_rows, query_out, weight_part

        backs, query_outs, weight_parts = lax.map(per_sequence, (inputs_s, grad_s, query_s, key_s, value_s, segments, positions))
        return backs, query_outs, jnp.sum(weight_parts, 0) / BATCH_COUNT

    backs, query_outs, weight_grad = lax.map(per_section, (layer_input, attn_grad, queries, keys, values, kv_weight))
    grad_prev = jnp.concatenate([backs[1:], jnp.zeros_like(backs[:1])], 0)
    return grad_prev, query_outs, weight_grad
```

```python
import functools
import math

import jax
import jax.numpy as jnp
import numpy as np
from jax import lax
from jax.experimental import pallas as pl
from jax.experimental.pallas import tpu as pltpu
from jax.sharding import PartitionSpec as P

QUERY_HEADS = 32
KEY_VALUE_HEADS = 4
HEAD_WIDTH = 128
QUERY_BLOCK = 256
MASKED = -1e30


def yarn_table(head_size):
    theta_base = 1000000.0
    factor = 4.0
    pretrain_len = 32768.0
    exponent = np.arange(0, head_size, 2) / head_size
    extrapolated = 1.0 / theta_base**exponent
    interpolated = extrapolated / factor

    def boundary(rotations):
        return (
            head_size
            * math.log(pretrain_len / (rotations * 2.0 * math.pi))
            / (2.0 * math.log(theta_base))
        )

    lower_dim = max(math.floor(boundary(32.0)), 0)
    upper_dim = min(math.ceil(boundary(1.0)), head_size - 1)
    ramp_width = max(upper_dim - lower_dim, 0.001)
    ramp_share = np.clip((np.arange(head_size // 2) - lower_dim) / ramp_width, 0.0, 1.0)
    keep_share = 1.0 - ramp_share
    frequency = interpolated * (1.0 - keep_share) + extrapolated * keep_share
    return (frequency.astype(np.float32), float(0.1 * math.log(factor) + 1.0))


def dot(a, b, dims):
    return lax.dot_general(a, b, (dims, ((), ())), preferred_element_type=jnp.float32)


NT = ((1,), (1,))
NN = ((1,), (0,))
TN = ((0,), (0,))
VMEM_LIMIT = 48 * 1024 * 1024


def rows_at(pos_ref, piece, count):
    return pl.ds(pl.multiple_of(pos_ref[piece] * count, count), count)


def attention_kernel(n, pos_ref, *refs):
    g_refs, kv_refs, refs = refs[:n], refs[n : 2 * n], refs[2 * n :]
    q_ref, seg_ref, cos_ref, sin_ref = refs[:4]
    dq_refs, dkv_ref = refs[4 : 4 + n], refs[4 + n]
    k_s, v_s, kt_s, bias_s, g_s, dq_s, dk_s, dv_s = refs[5 + n :]
    tokens = q_ref.shape[0]
    piece_rows = tokens // n
    width = HEAD_WIDTH
    half = width // 2
    block = min(QUERY_BLOCK, tokens)
    scale = HEAD_WIDTH ** (-0.5)
    head = pl.program_id(0)

    @pl.when(head == 0)
    def _():
        for m in range(n):
            rows = rows_at(pos_ref, m, piece_rows)
            k_s[rows, :] = kv_refs[m][:, :width]
            v_s[rows, :] = kv_refs[m][:, width:]
        kt_s[...] = k_s[...].astype(jnp.float32).T.astype(jnp.bfloat16)
        seg_row = seg_ref[...].astype(jnp.float32)
        seg_col = jnp.broadcast_to(seg_row, (width, tokens)).T
        for start in range(0, tokens, width):
            q_seg = seg_row[:, start : start + width]
            key_id = lax.broadcasted_iota(jnp.int32, (tokens, width), 0)
            query_id = start + lax.broadcasted_iota(jnp.int32, (tokens, width), 1)
            allowed = (seg_col == q_seg) & (key_id <= query_id)
            bias_s[:, start : start + width] = jnp.where(allowed, 0.0, MASKED)
        dk_s[...] = jnp.zeros_like(dk_s)
        dv_s[...] = jnp.zeros_like(dv_s)

    for m in range(n):
        g_s[rows_at(pos_ref, m, piece_rows), :] = g_refs[m][...]

    for start in range(0, tokens, block):
        stop = start + block
        q = q_ref[start:stop, :]
        g = g_s[start:stop, :]
        scores = dot(k_s[:stop, :], q, NT) * scale + bias_s[:stop, start:stop]
        top = jnp.max(scores, 0, keepdims=True)
        shifted = jnp.exp(scores - top)
        total = jnp.sum(shifted, 0, keepdims=True)
        attention = shifted * (1.0 / total)
        dprobs = dot(v_s[:stop, :], g, NT)
        delta = jnp.sum(attention * dprobs, 0, keepdims=True)
        dscores = (attention * (dprobs - delta)).astype(jnp.bfloat16)
        dv_s[:stop, :] += dot(attention.astype(jnp.bfloat16), g, NN)
        dk_s[:stop, :] += dot(dscores, q, NN)
        dq = dot(kt_s[:, :stop], dscores, NN)
        c = cos_ref[:, start:stop]
        t = sin_ref[:, start:stop]
        u, w = dq[:half], dq[half:]
        turned = jnp.concatenate([u * c + w * t, w * c - u * t], 0)
        dq_s[start:stop, :] = turned.T.astype(jnp.bfloat16)
    for m in range(n):
        dq_refs[m][...] = dq_s[rows_at(pos_ref, m, piece_rows), :]

    @pl.when(head == pl.num_programs(0) - 1)
    def _():
        dk = dk_s[...].T
        c = cos_ref[...]
        t = sin_ref[...]
        u, w = dk[:half], dk[half:]
        turned = jnp.concatenate([u * c + w * t, w * c - u * t], 0)
        dkv_ref[:, :width] = turned.T.astype(jnp.bfloat16)
        dkv_ref[:, width:] = dv_s[...].astype(jnp.bfloat16)


def attention_backward(pos, pieces, queries, segments, cosine, sine):
    n = len(pieces)
    tokens, cols = queries.shape
    width = HEAD_WIDTH
    heads = cols // width
    piece_rows = tokens // n
    bf16, f32 = jnp.bfloat16, jnp.float32
    out = pl.pallas_call(
        functools.partial(attention_kernel, n),
        out_shape=[jax.ShapeDtypeStruct((piece_rows, cols), bf16)] * n
        + [jax.ShapeDtypeStruct((tokens, 2 * width), bf16)],
        grid_spec=pltpu.PrefetchScalarGridSpec(
            num_scalar_prefetch=1,
            grid=(heads,),
            in_specs=[pl.BlockSpec((piece_rows, width), lambda h, p: (0, h))] * n
            + [pl.BlockSpec((piece_rows, 2 * width), lambda h, p: (0, cols // (2 * width)))] * n
            + [
                pl.BlockSpec((tokens, width), lambda h, p: (0, h)),
                pl.BlockSpec((1, tokens), lambda h, p: (0, 0)),
                pl.BlockSpec((width // 2, tokens), lambda h, p: (0, 0)),
                pl.BlockSpec((width // 2, tokens), lambda h, p: (0, 0)),
            ],
            out_specs=[pl.BlockSpec((piece_rows, width), lambda h, p: (0, h))] * n
            + [pl.BlockSpec((tokens, 2 * width), lambda h, p: (0, 0))],
            scratch_shapes=[
                pltpu.VMEM((tokens, width), bf16),
                pltpu.VMEM((tokens, width), bf16),
                pltpu.VMEM((width, tokens), bf16),
                pltpu.VMEM((tokens, tokens), f32),
                pltpu.VMEM((tokens, width), bf16),
                pltpu.VMEM((tokens, width), bf16),
                pltpu.VMEM((tokens, width), f32),
                pltpu.VMEM((tokens, width), f32),
            ],
        ),
        compiler_params=pltpu.CompilerParams(
            dimension_semantics=("arbitrary",), vmem_limit_bytes=VMEM_LIMIT
        ),
        cost_estimate=pl.CostEstimate(
            flops=10 * heads * tokens * tokens * width,
            bytes_accessed=6 * tokens * cols,
            transcendentals=heads * tokens * tokens,
        ),
        name="attention_backward",
    )(pos, *pieces, *pieces, queries, segments, cosine, sine)
    return out[:n], out[n]


def input_kernel(n, share, pos_ref, *refs):
    part_refs, weight_ref = refs[:n], refs[n]
    out_refs, kv_ref = refs[n + 1 : 2 * n + 1], refs[2 * n + 1]
    total = refs[2 * n + 2] if share > 1 else None
    width = HEAD_WIDTH
    kv_width = kv_ref.shape[1] // 2
    piece_rows = out_refs[0].shape[0]
    if share > 1:
        total[...] = jnp.zeros_like(total)
    for m in range(n):
        head = pos_ref[m] // share
        for side in range(2):
            cols = pl.ds(pl.multiple_of(side * kv_width + head * width, width), width)
            part = part_refs[m][:, side * width : (side + 1) * width]
            if share > 1:
                total[:, cols] += part.astype(jnp.float32)
            else:
                kv_ref[:, cols] = part
    if share > 1:
        kv_ref[...] = total[...].astype(kv_ref.dtype)
    for m in range(n):
        rows = kv_ref[rows_at(pos_ref, m, piece_rows), :]
        out_refs[m][...] = dot(rows, weight_ref[...], NT).astype(jnp.bfloat16)


def input_gradient(pos, parts, weight, share):
    n = len(parts)
    tokens = parts[0].shape[0]
    rows, cols = weight.shape
    bf16 = jnp.bfloat16
    vmem = pl.BlockSpec(memory_space=pltpu.VMEM)
    out = pl.pallas_call(
        functools.partial(input_kernel, n, share),
        out_shape=[jax.ShapeDtypeStruct((tokens // n, rows), bf16)] * n
        + [jax.ShapeDtypeStruct((tokens, cols), bf16)],
        in_specs=[pl.BlockSpec(memory_space=pltpu.SMEM)] + [vmem] * (n + 1),
        out_specs=[vmem] * (n + 1),
        scratch_shapes=[pltpu.VMEM((tokens, cols), jnp.float32)] if share > 1 else [],
        compiler_params=pltpu.CompilerParams(vmem_limit_bytes=VMEM_LIMIT),
        cost_estimate=pl.CostEstimate(
            flops=2 * tokens * rows * cols,
            bytes_accessed=2 * (2 * tokens * cols + rows * cols + tokens * rows),
            transcendentals=0,
        ),
        name="input_gradient",
    )(pos, *parts, weight)
    return out[:n], out[n]


def weight_kernel(n, halves, pos_ref, *refs):
    x_refs, kv_ref = refs[:n], refs[n]
    out_refs, x_s = refs[n + 1 : -1], refs[-1]
    piece_rows = x_refs[0].shape[0]
    for m in range(n):
        x_s[rows_at(pos_ref, m, piece_rows), :] = x_refs[m][...]
    if halves:
        cols = kv_ref.shape[1] // 2
        mine = pos_ref[n]
        for out_ref, side in zip(out_refs, (1 - mine, mine)):
            picked = kv_ref[:, pl.ds(pl.multiple_of(side * cols, cols), cols)]
            out_ref[...] = dot(x_s[...], picked, TN).astype(out_ref.dtype)
    else:
        out_refs[0][...] = dot(x_s[...], kv_ref[...], TN)


def weight_gradient(pos, pieces, kv_grad, halves):
    n = len(pieces)
    rows = pieces[0].shape[1]
    tokens, cols = kv_grad.shape
    vmem = pl.BlockSpec(memory_space=pltpu.VMEM)
    if halves:
        out_shape = [
            jax.ShapeDtypeStruct((rows, cols // 2), jnp.bfloat16),
            jax.ShapeDtypeStruct((rows, cols // 2), jnp.float32),
        ]
    else:
        out_shape = [jax.ShapeDtypeStruct((rows, cols), jnp.float32)]
    return pl.pallas_call(
        functools.partial(weight_kernel, n, halves),
        out_shape=out_shape,
        in_specs=[pl.BlockSpec(memory_space=pltpu.SMEM)] + [vmem] * (n + 1),
        out_specs=[vmem] * len(out_shape),
        scratch_shapes=[pltpu.VMEM((tokens, rows), jnp.bfloat16)],
        compiler_params=pltpu.CompilerParams(vmem_limit_bytes=VMEM_LIMIT),
        cost_estimate=pl.CostEstimate(
            flops=2 * tokens * rows * cols,
            bytes_accessed=2 * tokens * (rows + cols) + 4 * rows * cols,
            transcendentals=0,
        ),
        name="weight_gradient",
    )(pos, *pieces, kv_grad)


def join_kernel(n, pos_ref, *refs):
    out_ref = refs[n]
    cols = refs[0].shape[1]
    for m in range(n):
        at = pl.ds(pl.multiple_of(pos_ref[m] * cols, cols), cols)
        out_ref[:, at] = refs[m][...]


def join_columns(pos, pieces):
    n = len(pieces)
    rows, cols = pieces[0].shape
    vmem = pl.BlockSpec(memory_space=pltpu.VMEM)
    return pl.pallas_call(
        functools.partial(join_kernel, n),
        out_shape=jax.ShapeDtypeStruct((rows, n * cols), pieces[0].dtype),
        in_specs=[pl.BlockSpec(memory_space=pltpu.SMEM)] + [vmem] * n,
        out_specs=vmem,
        compiler_params=pltpu.CompilerParams(vmem_limit_bytes=VMEM_LIMIT),
        cost_estimate=pl.CostEstimate(
            flops=0, bytes_accessed=4 * rows * n * cols, transcendentals=0
        ),
        name="join_columns",
    )(pos, *pieces)


def swapped(value, mask, axis="ctx"):
    size = lax.axis_size(axis)
    return lax.ppermute(value, axis, [(i, i ^ mask) for i in range(size)])


def to_section_before(value, mask):
    sections, size = lax.axis_size("section"), lax.axis_size("ctx")
    pairs = [
        (s * size + i, (s - 1) * size + (i ^ mask)) for s in range(1, sections) for i in range(size)
    ]
    return lax.ppermute(value, ("section", "ctx"), pairs)


def after(values, others):
    return lax.optimization_barrier((values, others))[0]


def on_device(layer_input, attn_grad, queries, keys, values, kv_weight, segments, positions):
    frequency, mscale = yarn_table(HEAD_WIDTH)
    width = HEAD_WIDTH
    inputs, grads = layer_input[0, 0], attn_grad[0, 0]
    key_rows, value_rows = keys[0, 0], values[0, 0]
    n = lax.axis_size("ctx")
    me = lax.axis_index("ctx")
    data_size = lax.axis_size("dp")
    tokens, cols = queries.shape[2:]
    kv_heads = key_rows.shape[1] // width
    share = n // kv_heads
    masks = list(range(1, n))[::-1]
    block_of = [me ^ m for m in range(n)]
    pos = jnp.stack([*block_of, lax.axis_index("dp")]).astype(jnp.int32)

    def block(array, at, size):
        return lax.dynamic_slice_in_dim(array, at * size, size, 1)

    def outgoing(m):
        head = block_of[m] // share
        return jnp.concatenate(
            [
                block(grads, block_of[m], cols),
                block(key_rows, head, width),
                block(value_rows, head, width),
            ],
            1,
        )

    sent = {m: swapped(outgoing(m), m) for m in masks}
    pieces = [outgoing(0), *(sent[m] for m in range(1, n))]

    angles = frequency[:, None] * positions.astype(jnp.float32)
    score_scale = width ** (-0.5)
    cosine = jnp.cos(angles) * (mscale * score_scale)
    sine = jnp.sin(angles) * (mscale * score_scale)

    features = inputs.shape[1] // n
    x_out = [block(inputs, block_of[m], features) for m in range(n)]
    x_held = after(x_out, pieces)
    x_sent = {m: swapped(x_held[m], m) for m in masks}
    x_pieces = [x_out[0], *(x_sent[m] for m in range(1, n))]

    dq_pieces, dkv = attention_backward(pos, pieces, queries[0, 0], segments, cosine, sine)

    parts = {0: dkv}
    bit = n // 2
    while bit:
        for m in sorted(parts):
            parts[m | bit] = swapped(parts[m], bit)
        bit //= 2
    parts = [parts[m] for m in range(n)]

    in_grads, kv_grad = input_gradient(pos, parts, kv_weight[0], share)
    in_sent = {m: to_section_before(in_grads[m], m) for m in [*masks, 0]}
    dq_held = after(dq_pieces, parts)
    dq_sent = {m: swapped(dq_held[m], m) for m in masks}

    halves = data_size == 2
    if halves:
        away, home = weight_gradient(pos, x_pieces, kv_grad, True)
        weight_grad = (home + swapped(away, 1, "dp").astype(jnp.float32)) / data_size
    else:
        (rows_part,) = weight_gradient(pos, x_pieces, kv_grad, False)
        weight_grad = lax.psum_scatter(rows_part, "dp", scatter_dimension=1, tiled=True) / data_size

    grad_prev = join_columns(pos, [in_sent[m] for m in range(n)])
    query_grad = join_columns(pos, [dq_pieces[0], *(dq_sent[m] for m in range(1, n))])
    return (grad_prev[None, None], query_grad[None, None], weight_grad[None])


def solution(mesh):
    return jax.shard_map(
        on_device,
        mesh=mesh,
        in_specs=(
            P("section", "dp", "ctx", None),
            P("section", "dp", "ctx", None),
            P("section", "dp", None, "ctx"),
            P("section", "dp", "ctx", None),
            P("section", "dp", "ctx", None),
            P("section", "ctx", None),
            P("dp", None),
            P("dp", None),
        ),
        out_specs=(
            P("section", "dp", "ctx", None),
            P("section", "dp", "ctx", None),
            P("section", "ctx", "dp"),
        ),
        check_vma=False,
    )
```

```python
import functools
import math

import jax
import jax.numpy as jnp
import numpy as np
from jax import lax
from jax.experimental import pallas as pl
from jax.experimental.pallas import tpu as pltpu
from jax.sharding import PartitionSpec as P

QUERY_HEADS = 32
KEY_VALUE_HEADS = 4
HEAD_WIDTH = 128
QUERY_BLOCK = 256
FEATURE_BLOCK = 256
MASKED = -1e30


def yarn_table(head_size):
    theta_base = 1000000.0
    factor = 4.0
    pretrain_len = 32768.0
    exponent = np.arange(0, head_size, 2) / head_size
    extrapolated = 1.0 / theta_base**exponent
    interpolated = extrapolated / factor

    def boundary(rotations):
        return (
            head_size
            * math.log(pretrain_len / (rotations * 2.0 * math.pi))
            / (2.0 * math.log(theta_base))
        )

    lower_dim = max(math.floor(boundary(32.0)), 0)
    upper_dim = min(math.ceil(boundary(1.0)), head_size - 1)
    ramp_width = max(upper_dim - lower_dim, 0.001)
    ramp_share = np.clip((np.arange(head_size // 2) - lower_dim) / ramp_width, 0.0, 1.0)
    keep_share = 1.0 - ramp_share
    frequency = interpolated * (1.0 - keep_share) + extrapolated * keep_share
    return (frequency.astype(np.float32), float(0.1 * math.log(factor) + 1.0))


def dot(a, b, dims):
    return lax.dot_general(a, b, (dims, ((), ())), preferred_element_type=jnp.float32)


NT = ((1,), (1,))
NN = ((1,), (0,))
TN = ((0,), (0,))
ATTENTION_VMEM = 24 * 1024 * 1024
VMEM_LIMIT = 24 * 1024 * 1024


def rows_at(pos_ref, piece, count):
    return pl.ds(pl.multiple_of(pos_ref[piece] * count, count), count)


def attention_kernel(n, pos_ref, *refs):
    g_refs, kv_refs, refs = refs[:n], refs[n : 2 * n], refs[2 * n :]
    q_ref, seg_ref, cos_ref, sin_ref = refs[:4]
    dq_ref, dkv_ref = refs[4:6]
    k_s, v_s, kt_s, bias_s, g_s, dk_s, dv_s = refs[6:]
    tokens = q_ref.shape[0]
    piece_rows = tokens // n
    width = HEAD_WIDTH
    half = width // 2
    block = min(QUERY_BLOCK, tokens)
    scale = HEAD_WIDTH ** (-0.5)
    head = pl.program_id(0)

    @pl.when(head == 0)
    def _():
        for m in range(n):
            rows = rows_at(pos_ref, m, piece_rows)
            k_s[rows, :] = kv_refs[m][:, :width]
            v_s[rows, :] = kv_refs[m][:, width:]
        kt_s[...] = k_s[...].astype(jnp.float32).T.astype(jnp.bfloat16)
        seg_row = seg_ref[...].astype(jnp.float32)
        seg_col = jnp.broadcast_to(seg_row, (width, tokens)).T
        for start in range(0, tokens, width):
            q_seg = seg_row[:, start : start + width]
            key_id = lax.broadcasted_iota(jnp.int32, (tokens, width), 0)
            query_id = start + lax.broadcasted_iota(jnp.int32, (tokens, width), 1)
            allowed = (seg_col == q_seg) & (key_id <= query_id)
            bias_s[:, start : start + width] = jnp.where(allowed, 0.0, MASKED)
        dk_s[...] = jnp.zeros_like(dk_s)
        dv_s[...] = jnp.zeros_like(dv_s)

    for m in range(n):
        g_s[rows_at(pos_ref, m, piece_rows), :] = g_refs[m][...]

    for start in range(0, tokens, block):
        stop = start + block
        q = q_ref[start:stop, :]
        g = g_s[start:stop, :]
        scores = dot(k_s[:stop, :], q, NT) * scale + bias_s[:stop, start:stop]
        top = jnp.max(scores, 0, keepdims=True)
        shifted = jnp.exp(scores - top)
        total = jnp.sum(shifted, 0, keepdims=True)
        attention = shifted * (1.0 / total)
        dprobs = dot(v_s[:stop, :], g, NT)
        delta = jnp.sum(attention * dprobs, 0, keepdims=True)
        dscores = (attention * (dprobs - delta)).astype(jnp.bfloat16)
        dv_s[:stop, :] += dot(attention.astype(jnp.bfloat16), g, NN)
        dk_s[:stop, :] += dot(dscores, q, NN)
        dq = dot(kt_s[:, :stop], dscores, NN)
        c = cos_ref[:, start:stop]
        t = sin_ref[:, start:stop]
        u, w = dq[:half], dq[half:]
        turned = jnp.concatenate([u * c + w * t, w * c - u * t], 0)
        dq_ref[start:stop, :] = turned.T.astype(jnp.bfloat16)

    @pl.when(head == pl.num_programs(0) - 1)
    def _():
        dk = dk_s[...].T
        c = cos_ref[...]
        t = sin_ref[...]
        u, w = dk[:half], dk[half:]
        turned = jnp.concatenate([u * c + w * t, w * c - u * t], 0)
        dkv_ref[:, :width] = turned.T.astype(jnp.bfloat16)
        dkv_ref[:, width:] = dv_s[...].astype(jnp.bfloat16)


def attention_backward(pos, pieces, queries, segments, cosine, sine):
    n = len(pieces)
    tokens, cols = queries.shape
    width = HEAD_WIDTH
    heads = cols // width
    piece_rows = tokens // n
    bf16, f32 = jnp.bfloat16, jnp.float32
    return pl.pallas_call(
        functools.partial(attention_kernel, n),
        out_shape=[
            jax.ShapeDtypeStruct((tokens, cols), bf16),
            jax.ShapeDtypeStruct((tokens, 2 * width), bf16),
        ],
        grid_spec=pltpu.PrefetchScalarGridSpec(
            num_scalar_prefetch=1,
            grid=(heads,),
            in_specs=[pl.BlockSpec((piece_rows, width), lambda h, p: (0, h))] * n
            + [pl.BlockSpec((piece_rows, 2 * width), lambda h, p: (0, cols // (2 * width)))] * n
            + [
                pl.BlockSpec((tokens, width), lambda h, p: (0, h)),
                pl.BlockSpec((1, tokens), lambda h, p: (0, 0)),
                pl.BlockSpec((width // 2, tokens), lambda h, p: (0, 0)),
                pl.BlockSpec((width // 2, tokens), lambda h, p: (0, 0)),
            ],
            out_specs=[
                pl.BlockSpec((tokens, width), lambda h, p: (0, h)),
                pl.BlockSpec((tokens, 2 * width), lambda h, p: (0, 0)),
            ],
            scratch_shapes=[
                pltpu.VMEM((tokens, width), bf16),
                pltpu.VMEM((tokens, width), bf16),
                pltpu.VMEM((width, tokens), bf16),
                pltpu.VMEM((tokens, tokens), f32),
                pltpu.VMEM((tokens, width), bf16),
                pltpu.VMEM((tokens, width), f32),
                pltpu.VMEM((tokens, width), f32),
            ],
        ),
        compiler_params=pltpu.CompilerParams(
            dimension_semantics=("arbitrary",), vmem_limit_bytes=ATTENTION_VMEM
        ),
        cost_estimate=pl.CostEstimate(
            flops=10 * heads * tokens * tokens * width,
            bytes_accessed=6 * tokens * cols,
            transcendentals=heads * tokens * tokens,
        ),
        name="attention_backward",
    )(pos, *pieces, *pieces, queries, segments, cosine, sine)


def input_kernel(n, share, pos_ref, *refs):
    part_refs, weight_ref = refs[:n], refs[n]
    out_refs, kv_ref = refs[n + 1 : 2 * n + 1], refs[2 * n + 1]
    weight_s, arrived, *sums = refs[2 * n + 2 :]
    total = sums[0] if share > 1 else kv_ref
    width = HEAD_WIDTH
    kv_width = kv_ref.shape[1] // 2
    piece_rows = out_refs[0].shape[0]
    blocks, block = weight_s.shape[:2]
    copies = [
        pltpu.make_async_copy(
            weight_ref.at[pl.ds(b * block, block), :], weight_s.at[b], arrived.at[b]
        )
        for b in range(blocks)
    ]
    for copy in copies:
        copy.start()
    if share > 1:
        total[...] = jnp.zeros_like(total)
    for m in range(n):
        head = pos_ref[m] // share
        for side in range(2):
            cols = pl.ds(pl.multiple_of(side * kv_width + head * width, width), width)
            part = part_refs[m][:, side * width : (side + 1) * width]
            if share > 1:
                total[:, cols] += part.astype(jnp.float32)
            else:
                total[:, cols] = part
    if share > 1:
        kv_ref[...] = total[...].astype(kv_ref.dtype)
    for b, copy in enumerate(copies):
        copy.wait()
        for m in range(n):
            rows = kv_ref[rows_at(pos_ref, m, piece_rows), :]
            out_refs[m][:, b * block : (b + 1) * block] = dot(rows, weight_s[b], NT).astype(
                jnp.bfloat16
            )


def input_gradient(pos, parts, weight, share):
    n = len(parts)
    tokens = parts[0].shape[0]
    rows, cols = weight.shape
    bf16 = jnp.bfloat16
    block = min(FEATURE_BLOCK, rows)
    vmem = pl.BlockSpec(memory_space=pltpu.VMEM)
    out = pl.pallas_call(
        functools.partial(input_kernel, n, share),
        out_shape=[jax.ShapeDtypeStruct((tokens // n, rows), bf16)] * n
        + [jax.ShapeDtypeStruct((tokens, cols), bf16)],
        in_specs=[pl.BlockSpec(memory_space=pltpu.SMEM)]
        + [vmem] * n
        + [pl.BlockSpec(memory_space=pltpu.HBM)],
        out_specs=[vmem] * (n + 1),
        scratch_shapes=[
            pltpu.VMEM((rows // block, block, cols), bf16),
            pltpu.SemaphoreType.DMA((rows // block,)),
        ]
        + ([pltpu.VMEM((tokens, cols), jnp.float32)] if share > 1 else []),
        compiler_params=pltpu.CompilerParams(vmem_limit_bytes=VMEM_LIMIT),
        cost_estimate=pl.CostEstimate(
            flops=2 * tokens * rows * cols,
            bytes_accessed=2 * (2 * tokens * cols + rows * cols + tokens * rows),
            transcendentals=0,
        ),
        name="input_gradient",
    )(pos, *parts, weight)
    return out[:n], out[n]


def weight_kernel(n, halves, pos_ref, *refs):
    x_refs, kv_ref = refs[:n], refs[n]
    out_refs, x_s = refs[n + 1 : -1], refs[-1]
    piece_rows = x_refs[0].shape[0]
    for m in range(n):
        x_s[rows_at(pos_ref, m, piece_rows), :] = x_refs[m][...]
    if halves:
        cols = kv_ref.shape[1] // 2
        mine = pos_ref[n]
        for out_ref, side in zip(out_refs, (1 - mine, mine)):
            picked = kv_ref[:, pl.ds(pl.multiple_of(side * cols, cols), cols)]
            out_ref[...] = dot(x_s[...], picked, TN).astype(out_ref.dtype)
    else:
        out_refs[0][...] = dot(x_s[...], kv_ref[...], TN)


def weight_gradient(pos, pieces, kv_grad, halves):
    n = len(pieces)
    rows = pieces[0].shape[1]
    tokens, cols = kv_grad.shape
    vmem = pl.BlockSpec(memory_space=pltpu.VMEM)
    if halves:
        out_shape = [
            jax.ShapeDtypeStruct((rows, cols // 2), jnp.bfloat16),
            jax.ShapeDtypeStruct((rows, cols // 2), jnp.float32),
        ]
    else:
        out_shape = [jax.ShapeDtypeStruct((rows, cols), jnp.float32)]
    return pl.pallas_call(
        functools.partial(weight_kernel, n, halves),
        out_shape=out_shape,
        in_specs=[pl.BlockSpec(memory_space=pltpu.SMEM)] + [vmem] * (n + 1),
        out_specs=[vmem] * len(out_shape),
        scratch_shapes=[pltpu.VMEM((tokens, rows), jnp.bfloat16)],
        compiler_params=pltpu.CompilerParams(vmem_limit_bytes=VMEM_LIMIT),
        cost_estimate=pl.CostEstimate(
            flops=2 * tokens * rows * cols,
            bytes_accessed=2 * tokens * (rows + cols) + 4 * rows * cols,
            transcendentals=0,
        ),
        name="weight_gradient",
    )(pos, *pieces, kv_grad)


def join_kernel(order, pos_ref, *refs):
    out_ref = refs[-1]
    n, cols = len(order), refs[0].shape[1]
    for i, m in enumerate(order):
        at = pl.ds(pl.multiple_of(pos_ref[m] * cols, cols), cols)
        if i == 0 and len(refs) > n + 1:
            relayed = pos_ref[n + 1] == 1

            @pl.when(relayed)
            def _():
                out_ref[:, at] = refs[n][...]

            @pl.when(jnp.logical_not(relayed))
            def _():
                out_ref[:, at] = refs[0][...]

        else:
            out_ref[:, at] = refs[i][...]


def join_columns(pos, order, pieces):
    rows, cols = pieces[0].shape
    n = len(order)
    vmem = pl.BlockSpec(memory_space=pltpu.VMEM)
    return pl.pallas_call(
        functools.partial(join_kernel, order),
        out_shape=jax.ShapeDtypeStruct((rows, n * cols), pieces[0].dtype),
        in_specs=[pl.BlockSpec(memory_space=pltpu.SMEM)] + [vmem] * len(pieces),
        out_specs=vmem,
        compiler_params=pltpu.CompilerParams(vmem_limit_bytes=VMEM_LIMIT),
        cost_estimate=pl.CostEstimate(
            flops=0, bytes_accessed=4 * rows * n * cols, transcendentals=0
        ),
        name="join_columns",
    )(pos, *pieces)


def lay_out_kernel(in_ref, out_ref):
    cols = in_ref.shape[2]
    for block in range(in_ref.shape[0]):
        out_ref[:, block * cols : (block + 1) * cols] = in_ref[block]


def lay_out(blocks):
    n, rows, cols = blocks.shape
    vmem = pl.BlockSpec(memory_space=pltpu.VMEM)
    return pl.pallas_call(
        lay_out_kernel,
        out_shape=jax.ShapeDtypeStruct((rows, n * cols), blocks.dtype),
        in_specs=[vmem],
        out_specs=vmem,
        compiler_params=pltpu.CompilerParams(vmem_limit_bytes=VMEM_LIMIT),
        cost_estimate=pl.CostEstimate(
            flops=0, bytes_accessed=4 * rows * n * cols, transcendentals=0
        ),
        name="lay_out",
    )(blocks)


def swapped(value, mask, axis="ctx"):
    size = lax.axis_size(axis)
    return lax.ppermute(value, axis, [(i, i ^ mask) for i in range(size)])


def to_section_before(value, mask):
    sections, size = lax.axis_size("section"), lax.axis_size("ctx")
    pairs = [
        (s * size + i, (s - 1) * size + (i ^ mask)) for s in range(1, sections) for i in range(size)
    ]
    return lax.ppermute(value, ("section", "ctx"), pairs)


def relayed_section_before(value, mask):
    sections, size = lax.axis_size("section"), lax.axis_size("ctx")
    half = sections // 2
    first = [
        (s * size + i, (s - 1) * size + (i if s == half else i ^ mask))
        for s in range(1, sections)
        for i in range(size)
    ]
    second = [((half - 1) * size + i, (half - 1) * size + (i ^ mask)) for i in range(size)]
    value = lax.ppermute(value, ("section", "ctx"), first)
    return value, lax.ppermute(value, ("section", "ctx"), second)


def after(values, others):
    return lax.optimization_barrier((values, others))[0]


def on_device(layer_input, attn_grad, queries, keys, values, kv_weight, segments, positions):
    frequency, mscale = yarn_table(HEAD_WIDTH)
    width = HEAD_WIDTH
    inputs, grads = layer_input[0, 0], attn_grad[0, 0]
    key_rows, value_rows = keys[0, 0], values[0, 0]
    n = lax.axis_size("ctx")
    me = lax.axis_index("ctx")
    data_size = lax.axis_size("dp")
    tokens, cols = queries.shape[2:]
    kv_heads = key_rows.shape[1] // width
    share = n // kv_heads
    masks = list(range(1, n))[::-1]
    block_of = [me ^ m for m in range(n)]
    section = lax.axis_index("section")
    relay = lax.axis_size("section") == 4 and n == 4
    at_relay = section == lax.axis_size("section") // 2 - 1
    pos = jnp.stack([*block_of, lax.axis_index("dp"), at_relay.astype(jnp.int32)])

    def block(array, at, size):
        return lax.dynamic_slice_in_dim(array, at * size, size, 1)

    def outgoing(m):
        head = block_of[m] // share
        return jnp.concatenate(
            [
                block(grads, block_of[m], cols),
                block(key_rows, head, width),
                block(value_rows, head, width),
            ],
            1,
        )

    sent = {m: swapped(outgoing(m), m) for m in masks}
    pieces = [outgoing(0), *(sent[m] for m in range(1, n))]

    angles = frequency[:, None] * positions.astype(jnp.float32)
    score_scale = width ** (-0.5)
    cosine = jnp.cos(angles) * (mscale * score_scale)
    sine = jnp.sin(angles) * (mscale * score_scale)

    features = inputs.shape[1] // n
    x_out = [block(inputs, block_of[m], features) for m in range(n)]
    far, near = n // 2, 1
    middle = [m for m in masks if m not in (far, near)]
    x_held = after(x_out, pieces)
    x_sent = {m: swapped(x_held[m], m) for m in [*middle, near]}

    dq, dkv = attention_backward(pos, pieces, queries[0, 0], segments, cosine, sine)
    dkv = after(dkv, x_sent)

    parts = {0: dkv}
    bit = far
    while bit:
        for m in sorted(parts):
            parts[m | bit] = swapped(parts[m], bit)
        bit //= 2
    x_sent[far] = swapped(after(x_out[far], parts[far]), far)
    dq = after(dq, parts[far])
    dq = lax.all_to_all(dq.reshape(n, tokens // n, cols), "ctx", 0, 0, tiled=True)
    parts = [parts[m] for m in range(n)]
    x_pieces = [x_out[0], *(x_sent[m] for m in range(1, n))]

    in_grads, kv_grad = input_gradient(pos, parts, kv_weight[0], share)
    order = [*masks, 0]
    in_sent = [to_section_before(in_grads[m], m) for m in order[1:]]
    if relay:
        direct, second = relayed_section_before(in_grads[order[0]], order[0])
        in_sent = [direct, *in_sent, second]
    else:
        in_sent = [to_section_before(in_grads[order[0]], order[0]), *in_sent]

    halves = data_size == 2
    if halves:
        away, home = weight_gradient(pos, x_pieces, kv_grad, True)
        weight_grad = (home + swapped(away, 1, "dp").astype(jnp.float32)) / data_size
    else:
        (rows_part,) = weight_gradient(pos, x_pieces, kv_grad, False)
        weight_grad = lax.psum_scatter(rows_part, "dp", scatter_dimension=1, tiled=True) / data_size

    query_grad = lay_out(dq)
    last = after(pos, (query_grad, weight_grad))
    grad_prev = join_columns(last, order, in_sent)
    return (grad_prev[None, None], query_grad[None, None], weight_grad[None])


def solution(mesh):
    return jax.shard_map(
        on_device,
        mesh=mesh,
        in_specs=(
            P("section", "dp", "ctx", None),
            P("section", "dp", "ctx", None),
            P("section", "dp", None, "ctx"),
            P("section", "dp", "ctx", None),
            P("section", "dp", "ctx", None),
            P("section", "ctx", None),
            P("dp", None),
            P("dp", None),
        ),
        out_specs=(
            P("section", "dp", "ctx", None),
            P("section", "dp", "ctx", None),
            P("section", "ctx", "dp"),
        ),
        check_vma=False,
    )
```

```python
import functools
import math

import jax
import jax.numpy as jnp
import numpy as np
from jax import lax
from jax.experimental import pallas as pl
from jax.experimental.pallas import tpu as pltpu
from jax.sharding import PartitionSpec as P

QUERY_HEADS = 32
KEY_VALUE_HEADS = 4
HEAD_WIDTH = 128
QUERY_BLOCK = 256
HEADS_AT_ONCE = 2
FEATURE_BLOCK = 256
MASKED = -1e30


def yarn_table(head_size):
    theta_base = 1000000.0
    factor = 4.0
    pretrain_len = 32768.0
    exponent = np.arange(0, head_size, 2) / head_size
    extrapolated = 1.0 / theta_base**exponent
    interpolated = extrapolated / factor

    def boundary(rotations):
        return (
            head_size
            * math.log(pretrain_len / (rotations * 2.0 * math.pi))
            / (2.0 * math.log(theta_base))
        )

    lower_dim = max(math.floor(boundary(32.0)), 0)
    upper_dim = min(math.ceil(boundary(1.0)), head_size - 1)
    ramp_width = max(upper_dim - lower_dim, 0.001)
    ramp_share = np.clip((np.arange(head_size // 2) - lower_dim) / ramp_width, 0.0, 1.0)
    keep_share = 1.0 - ramp_share
    frequency = interpolated * (1.0 - keep_share) + extrapolated * keep_share
    return (frequency.astype(np.float32), float(0.1 * math.log(factor) + 1.0))


def dot(a, b, dims):
    return lax.dot_general(a, b, (dims, ((), ())), preferred_element_type=jnp.float32)


NT = ((1,), (1,))
NN = ((1,), (0,))
TN = ((0,), (0,))
ATTENTION_VMEM = 24 * 1024 * 1024
VMEM_LIMIT = 24 * 1024 * 1024


def rows_at(pos_ref, piece, count):
    return pl.ds(pl.multiple_of(pos_ref[piece] * count, count), count)


def attention_kernel(n, pos_ref, *refs):
    g_refs, kv_refs, refs = refs[:n], refs[n : 2 * n], refs[2 * n :]
    q_ref, seg_ref, cos_ref, sin_ref = refs[:4]
    dq_ref, dkv_ref = refs[4:6]
    k_s, v_s, kt_s, bias_s, g_s, dk_s, dv_s = refs[6:]
    tokens = q_ref.shape[0]
    piece_rows = tokens // n
    width = HEAD_WIDTH
    half = width // 2
    block = min(QUERY_BLOCK, tokens)
    to_exponent = HEAD_WIDTH ** (-0.5) * math.log2(math.e)
    head = pl.program_id(0)

    @pl.when(head == 0)
    def _():
        for m in range(n):
            rows = rows_at(pos_ref, m, piece_rows)
            k_s[rows, :] = kv_refs[m][:, :width]
            v_s[rows, :] = kv_refs[m][:, width:]
        kt_s[...] = k_s[...].astype(jnp.float32).T.astype(jnp.bfloat16)
        seg_row = seg_ref[...].astype(jnp.float32)
        seg_col = jnp.broadcast_to(seg_row, (width, tokens)).T
        for start in range(0, tokens, width):
            q_seg = seg_row[:, start : start + width]
            key_id = lax.broadcasted_iota(jnp.int32, (tokens, width), 0)
            query_id = start + lax.broadcasted_iota(jnp.int32, (tokens, width), 1)
            allowed = (seg_col == q_seg) & (key_id <= query_id)
            bias_s[:, start : start + width] = jnp.where(allowed, 0.0, MASKED)
        dk_s[...] = jnp.zeros_like(dk_s)
        dv_s[...] = jnp.zeros_like(dv_s)

    for m in range(n):
        g_s[rows_at(pos_ref, m, piece_rows), :] = g_refs[m][...]

    for start in range(0, tokens, block):
        stop = start + block
        c = cos_ref[:, start:stop]
        t = sin_ref[:, start:stop]
        grad_k, grad_v = [], []
        for lane in range(0, g_s.shape[1], width):
            q = q_ref[start:stop, lane : lane + width]
            g = g_s[start:stop, lane : lane + width]
            scores = dot(k_s[:stop, :], q, NT) * to_exponent + bias_s[:stop, start:stop]
            top = jnp.max(scores, 0, keepdims=True)
            shifted = jnp.exp2(scores - top)
            total = jnp.sum(shifted, 0, keepdims=True)
            attention = shifted * (1.0 / total)
            dprobs = dot(v_s[:stop, :], g, NT)
            delta = jnp.sum(attention * dprobs, 0, keepdims=True)
            dscores = (attention * (dprobs - delta)).astype(jnp.bfloat16)
            grad_v.append(dot(attention.astype(jnp.bfloat16), g, NN))
            grad_k.append(dot(dscores, q, NN))
            dq = dot(kt_s[:, :stop], dscores, NN)
            u, w = dq[:half], dq[half:]
            turned = jnp.concatenate([u * c + w * t, w * c - u * t], 0)
            dq_ref[start:stop, lane : lane + width] = turned.T.astype(jnp.bfloat16)
        dv_s[:stop, :] += sum(grad_v[1:], grad_v[0])
        dk_s[:stop, :] += sum(grad_k[1:], grad_k[0])

    @pl.when(head == pl.num_programs(0) - 1)
    def _():
        dk = dk_s[...].T
        c = cos_ref[...]
        t = sin_ref[...]
        u, w = dk[:half], dk[half:]
        turned = jnp.concatenate([u * c + w * t, w * c - u * t], 0)
        dkv_ref[:, :width] = turned.T.astype(jnp.bfloat16)
        dkv_ref[:, width:] = dv_s[...].astype(jnp.bfloat16)


def attention_backward(pos, pieces, queries, segments, cosine, sine):
    n = len(pieces)
    tokens, cols = queries.shape
    width = HEAD_WIDTH
    heads = cols // width
    step = min(HEADS_AT_ONCE, heads) * width
    piece_rows = tokens // n
    bf16, f32 = jnp.bfloat16, jnp.float32
    return pl.pallas_call(
        functools.partial(attention_kernel, n),
        out_shape=[
            jax.ShapeDtypeStruct((tokens, cols), bf16),
            jax.ShapeDtypeStruct((tokens, 2 * width), bf16),
        ],
        grid_spec=pltpu.PrefetchScalarGridSpec(
            num_scalar_prefetch=1,
            grid=(cols // step,),
            in_specs=[pl.BlockSpec((piece_rows, step), lambda h, p: (0, h))] * n
            + [pl.BlockSpec((piece_rows, 2 * width), lambda h, p: (0, cols // (2 * width)))] * n
            + [
                pl.BlockSpec((tokens, step), lambda h, p: (0, h)),
                pl.BlockSpec((1, tokens), lambda h, p: (0, 0)),
                pl.BlockSpec((width // 2, tokens), lambda h, p: (0, 0)),
                pl.BlockSpec((width // 2, tokens), lambda h, p: (0, 0)),
            ],
            out_specs=[
                pl.BlockSpec((tokens, step), lambda h, p: (0, h)),
                pl.BlockSpec((tokens, 2 * width), lambda h, p: (0, 0)),
            ],
            scratch_shapes=[
                pltpu.VMEM((tokens, width), bf16),
                pltpu.VMEM((tokens, width), bf16),
                pltpu.VMEM((width, tokens), bf16),
                pltpu.VMEM((tokens, tokens), f32),
                pltpu.VMEM((tokens, step), bf16),
                pltpu.VMEM((tokens, width), f32),
                pltpu.VMEM((tokens, width), f32),
            ],
        ),
        compiler_params=pltpu.CompilerParams(
            dimension_semantics=("arbitrary",), vmem_limit_bytes=ATTENTION_VMEM
        ),
        cost_estimate=pl.CostEstimate(
            flops=10 * heads * tokens * tokens * width,
            bytes_accessed=6 * tokens * cols,
            transcendentals=heads * tokens * tokens,
        ),
        name="attention_backward",
    )(pos, *pieces, *pieces, queries, segments, cosine, sine)


def input_kernel(n, share, pos_ref, *refs):
    part_refs, weight_ref = refs[:n], refs[n]
    out_refs, kv_ref = refs[n + 1 : 2 * n + 1], refs[2 * n + 1]
    weight_s, arrived, *sums = refs[2 * n + 2 :]
    total = sums[0] if share > 1 else kv_ref
    width = HEAD_WIDTH
    kv_width = kv_ref.shape[1] // 2
    piece_rows = out_refs[0].shape[0]
    blocks, block = weight_s.shape[:2]
    copies = [
        pltpu.make_async_copy(
            weight_ref.at[pl.ds(b * block, block), :], weight_s.at[b], arrived.at[b]
        )
        for b in range(blocks)
    ]
    for copy in copies:
        copy.start()
    if share > 1:
        total[...] = jnp.zeros_like(total)
    for source in range(n):
        head = pos_ref[source] // share
        for m in range(n):
            rows = slice(m * piece_rows, (m + 1) * piece_rows)
            part = part_refs[source][rows_at(pos_ref, m, piece_rows), :]
            for side in range(2):
                cols = pl.ds(pl.multiple_of(side * kv_width + head * width, width), width)
                own = part[:, side * width : (side + 1) * width]
                if share > 1:
                    total[rows, cols] += own.astype(jnp.float32)
                else:
                    total[rows, cols] = own
    if share > 1:
        kv_ref[...] = total[...].astype(kv_ref.dtype)
    for b, copy in enumerate(copies):
        copy.wait()
        cols = slice(b * block, (b + 1) * block)
        product = dot(kv_ref[...], weight_s[b], NT).astype(jnp.bfloat16)
        for m in range(n):
            out_refs[m][:, cols] = product[m * piece_rows : (m + 1) * piece_rows]


def input_gradient(pos, parts, weight, share):
    n = len(parts)
    tokens = parts[0].shape[0]
    rows, cols = weight.shape
    bf16 = jnp.bfloat16
    block = min(FEATURE_BLOCK, rows)
    vmem = pl.BlockSpec(memory_space=pltpu.VMEM)
    out = pl.pallas_call(
        functools.partial(input_kernel, n, share),
        out_shape=[jax.ShapeDtypeStruct((tokens // n, rows), bf16)] * n
        + [jax.ShapeDtypeStruct((tokens, cols), bf16)],
        in_specs=[pl.BlockSpec(memory_space=pltpu.SMEM)]
        + [vmem] * n
        + [pl.BlockSpec(memory_space=pltpu.HBM)],
        out_specs=[vmem] * (n + 1),
        scratch_shapes=[
            pltpu.VMEM((rows // block, block, cols), bf16),
            pltpu.SemaphoreType.DMA((rows // block,)),
        ]
        + ([pltpu.VMEM((tokens, cols), jnp.float32)] if share > 1 else []),
        compiler_params=pltpu.CompilerParams(vmem_limit_bytes=VMEM_LIMIT),
        cost_estimate=pl.CostEstimate(
            flops=2 * tokens * rows * cols,
            bytes_accessed=2 * (2 * tokens * cols + rows * cols + tokens * rows),
            transcendentals=0,
        ),
        name="input_gradient",
    )(pos, *parts, pltpu.with_memory_space_constraint(weight, pltpu.HBM))
    return out[:n], out[n]


def weight_kernel(n, halves, pos_ref, *refs):
    x_refs, kv_ref = refs[:n], refs[n]
    out_refs, x_s = refs[n + 1 : -1], refs[-1]
    piece_rows = x_refs[0].shape[0]
    for m in range(n):
        x_s[m * piece_rows : (m + 1) * piece_rows, :] = x_refs[m][...]
    if halves:
        cols = kv_ref.shape[1] // 2
        mine = pos_ref[n]
        for out_ref, side in zip(out_refs, (1 - mine, mine)):
            picked = kv_ref[:, pl.ds(pl.multiple_of(side * cols, cols), cols)]
            out_ref[...] = dot(x_s[...], picked, TN).astype(out_ref.dtype)
    else:
        out_refs[0][...] = dot(x_s[...], kv_ref[...], TN)


def weight_gradient(pos, pieces, kv_grad, halves):
    n = len(pieces)
    rows = pieces[0].shape[1]
    tokens, cols = kv_grad.shape
    vmem = pl.BlockSpec(memory_space=pltpu.VMEM)
    if halves:
        out_shape = [
            jax.ShapeDtypeStruct((rows, cols // 2), jnp.bfloat16),
            jax.ShapeDtypeStruct((rows, cols // 2), jnp.float32),
        ]
    else:
        out_shape = [jax.ShapeDtypeStruct((rows, cols), jnp.float32)]
    return pl.pallas_call(
        functools.partial(weight_kernel, n, halves),
        out_shape=out_shape,
        in_specs=[pl.BlockSpec(memory_space=pltpu.SMEM)] + [vmem] * (n + 1),
        out_specs=[vmem] * len(out_shape),
        scratch_shapes=[pltpu.VMEM((tokens, rows), jnp.bfloat16)],
        compiler_params=pltpu.CompilerParams(vmem_limit_bytes=VMEM_LIMIT),
        cost_estimate=pl.CostEstimate(
            flops=2 * tokens * rows * cols,
            bytes_accessed=2 * tokens * (rows + cols) + 4 * rows * cols,
            transcendentals=0,
        ),
        name="weight_gradient",
    )(pos, *pieces, kv_grad)


def join_kernel(order, pos_ref, *refs):
    out_ref = refs[-1]
    n, cols = len(order), refs[0].shape[1]
    for i, m in enumerate(order):
        at = pl.ds(pl.multiple_of(pos_ref[m] * cols, cols), cols)
        if i == 0 and len(refs) > n + 1:
            relayed = pos_ref[n + 1] == 1

            @pl.when(relayed)
            def _():
                out_ref[:, at] = refs[n][...]

            @pl.when(jnp.logical_not(relayed))
            def _():
                out_ref[:, at] = refs[0][...]

        else:
            out_ref[:, at] = refs[i][...]


def join_columns(pos, order, pieces):
    rows, cols = pieces[0].shape
    n = len(order)
    vmem = pl.BlockSpec(memory_space=pltpu.VMEM)
    return pl.pallas_call(
        functools.partial(join_kernel, order),
        out_shape=jax.ShapeDtypeStruct((rows, n * cols), pieces[0].dtype),
        in_specs=[pl.BlockSpec(memory_space=pltpu.SMEM)] + [vmem] * len(pieces),
        out_specs=vmem,
        compiler_params=pltpu.CompilerParams(vmem_limit_bytes=VMEM_LIMIT),
        cost_estimate=pl.CostEstimate(
            flops=0, bytes_accessed=4 * rows * n * cols, transcendentals=0
        ),
        name="join_columns",
    )(pos, *pieces)


def lay_out_kernel(in_ref, out_ref):
    cols = in_ref.shape[2]
    for block in range(in_ref.shape[0]):
        out_ref[:, block * cols : (block + 1) * cols] = in_ref[block]


def lay_out(blocks):
    n, rows, cols = blocks.shape
    vmem = pl.BlockSpec(memory_space=pltpu.VMEM)
    return pl.pallas_call(
        lay_out_kernel,
        out_shape=jax.ShapeDtypeStruct((rows, n * cols), blocks.dtype),
        in_specs=[vmem],
        out_specs=vmem,
        compiler_params=pltpu.CompilerParams(vmem_limit_bytes=VMEM_LIMIT),
        cost_estimate=pl.CostEstimate(
            flops=0, bytes_accessed=4 * rows * n * cols, transcendentals=0
        ),
        name="lay_out",
    )(blocks)


def swapped(value, mask, axis="ctx"):
    size = lax.axis_size(axis)
    return lax.ppermute(value, axis, [(i, i ^ mask) for i in range(size)])


def to_section_before(value, mask):
    sections, size = lax.axis_size("section"), lax.axis_size("ctx")
    pairs = [
        (s * size + i, (s - 1) * size + (i ^ mask)) for s in range(1, sections) for i in range(size)
    ]
    return lax.ppermute(value, ("section", "ctx"), pairs)


def relayed_section_before(value, mask):
    sections, size = lax.axis_size("section"), lax.axis_size("ctx")
    half = sections // 2
    first = [
        (s * size + i, (s - 1) * size + (i if s == half else i ^ mask))
        for s in range(1, sections)
        for i in range(size)
    ]
    second = [((half - 1) * size + i, (half - 1) * size + (i ^ mask)) for i in range(size)]
    value = lax.ppermute(value, ("section", "ctx"), first)
    return value, lax.ppermute(value, ("section", "ctx"), second)


def after(values, others):
    return lax.optimization_barrier((values, others))[0]


def on_device(layer_input, attn_grad, queries, keys, values, kv_weight, segments, positions):
    frequency, mscale = yarn_table(HEAD_WIDTH)
    width = HEAD_WIDTH
    inputs, grads = layer_input[0, 0], attn_grad[0, 0]
    key_rows, value_rows = keys[0, 0], values[0, 0]
    n = lax.axis_size("ctx")
    me = lax.axis_index("ctx")
    data_size = lax.axis_size("dp")
    tokens, cols = queries.shape[2:]
    kv_heads = key_rows.shape[1] // width
    share = n // kv_heads
    masks = list(range(1, n))[::-1]
    block_of = [me ^ m for m in range(n)]
    section = lax.axis_index("section")
    relay = lax.axis_size("section") == 4 and n == 4
    at_relay = section == lax.axis_size("section") // 2 - 1
    pos = jnp.stack([*block_of, lax.axis_index("dp"), at_relay.astype(jnp.int32)])

    def block(array, at, size):
        return lax.dynamic_slice_in_dim(array, at * size, size, 1)

    def outgoing(m):
        head = block_of[m] // share
        return jnp.concatenate(
            [
                block(grads, block_of[m], cols),
                block(key_rows, head, width),
                block(value_rows, head, width),
            ],
            1,
        )

    sent = {m: swapped(outgoing(m), m) for m in masks}
    pieces = [outgoing(0), *(sent[m] for m in range(1, n))]

    angles = frequency[:, None] * positions.astype(jnp.float32)
    score_scale = width ** (-0.5)
    cosine = jnp.cos(angles) * (mscale * score_scale)
    sine = jnp.sin(angles) * (mscale * score_scale)

    features = inputs.shape[1] // n
    x_out = [block(inputs, block_of[m], features) for m in range(n)]
    far, near = n // 2, 1
    middle = [m for m in masks if m not in (far, near)]
    x_held = after(x_out, pieces)
    x_sent = {m: swapped(x_held[m], m) for m in [*middle, far]}
    x_sent[near] = swapped(x_out[near], near)

    dq, dkv = attention_backward(pos, pieces, queries[0, 0], segments, cosine, sine)
    dkv = after(dkv, [x_sent[m] for m in [near, *middle]])

    parts = {0: dkv}
    bit = far
    while bit:
        for m in sorted(parts):
            held = after(parts[m], x_sent) if m else parts[m]
            parts[m | bit] = swapped(held, bit)
        bit //= 2
    dq = after(dq, parts[far])
    dq = lax.all_to_all(dq.reshape(n, tokens // n, cols), "ctx", 0, 0, tiled=True)
    parts = [parts[m] for m in range(n)]
    x_pieces = [x_out[0], *(x_sent[m] for m in range(1, n))]

    in_grads, kv_grad = input_gradient(pos, parts, kv_weight[0], share)
    order = [*masks, 0]
    in_sent = [to_section_before(in_grads[m], m) for m in order[1:]]
    if relay:
        direct, second = relayed_section_before(in_grads[order[0]], order[0])
        in_sent = [direct, *in_sent, second]
    else:
        in_sent = [to_section_before(in_grads[order[0]], order[0]), *in_sent]

    halves = data_size == 2
    if halves:
        away, home = weight_gradient(pos, x_pieces, kv_grad, True)
        weight_grad = (home + swapped(away, 1, "dp").astype(jnp.float32)) / data_size
    else:
        (rows_part,) = weight_gradient(pos, x_pieces, kv_grad, False)
        weight_grad = lax.psum_scatter(rows_part, "dp", scatter_dimension=1, tiled=True) / data_size

    query_grad = lay_out(dq)
    last = after(pos, (query_grad, weight_grad))
    grad_prev = join_columns(last, order, in_sent)
    return (grad_prev[None, None], query_grad[None, None], weight_grad[None])


def solution(mesh):
    return jax.shard_map(
        on_device,
        mesh=mesh,
        in_specs=(
            P("section", "dp", "ctx", None),
            P("section", "dp", "ctx", None),
            P("section", "dp", None, "ctx"),
            P("section", "dp", "ctx", None),
            P("section", "dp", "ctx", None),
            P("section", "ctx", None),
            P("dp", None),
            P("dp", None),
        ),
        out_specs=(
            P("section", "dp", "ctx", None),
            P("section", "dp", "ctx", None),
            P("section", "ctx", "dp"),
        ),
        check_vma=False,
    )
```

```python
import functools
import math

import jax
import jax.numpy as jnp
import numpy as np
from jax import lax
from jax.experimental import pallas as pl
from jax.experimental.pallas import tpu as pltpu
from jax.sharding import PartitionSpec as P

QUERY_HEADS = 32
KEY_VALUE_HEADS = 4
HEAD_WIDTH = 128
QUERY_BLOCK = 256
HEADS_AT_ONCE = 2
FEATURE_BLOCK = 256
MASKED = -1e30


def yarn_table(head_size):
    theta_base = 1000000.0
    factor = 4.0
    pretrain_len = 32768.0
    exponent = np.arange(0, head_size, 2) / head_size
    extrapolated = 1.0 / theta_base**exponent
    interpolated = extrapolated / factor

    def boundary(rotations):
        return (
            head_size
            * math.log(pretrain_len / (rotations * 2.0 * math.pi))
            / (2.0 * math.log(theta_base))
        )

    lower_dim = max(math.floor(boundary(32.0)), 0)
    upper_dim = min(math.ceil(boundary(1.0)), head_size - 1)
    ramp_width = max(upper_dim - lower_dim, 0.001)
    ramp_share = np.clip((np.arange(head_size // 2) - lower_dim) / ramp_width, 0.0, 1.0)
    keep_share = 1.0 - ramp_share
    frequency = interpolated * (1.0 - keep_share) + extrapolated * keep_share
    return (frequency.astype(np.float32), float(0.1 * math.log(factor) + 1.0))


def dot(a, b, dims):
    return lax.dot_general(a, b, (dims, ((), ())), preferred_element_type=jnp.float32)


NT = ((1,), (1,))
NN = ((1,), (0,))
TN = ((0,), (0,))
ATTENTION_VMEM = 24 * 1024 * 1024
VMEM_LIMIT = 24 * 1024 * 1024


def rows_at(pos_ref, piece, count):
    return pl.ds(pl.multiple_of(pos_ref[piece] * count, count), count)


def attention_kernel(n, pos_ref, *refs):
    g_refs, kv_refs, refs = refs[:n], refs[n : 2 * n], refs[2 * n :]
    q_ref, seg_ref, cos_ref, sin_ref = refs[:4]
    dq_ref, dkv_ref = refs[4:6]
    k_s, v_s, kt_s, bias_s, g_s, dk_s, dv_s = refs[6:]
    tokens = q_ref.shape[0]
    piece_rows = tokens // n
    width = HEAD_WIDTH
    half = width // 2
    block = min(QUERY_BLOCK, tokens)
    to_exponent = HEAD_WIDTH ** (-0.5) * math.log2(math.e)
    head = pl.program_id(0)

    @pl.when(head == 0)
    def _():
        for m in range(n):
            rows = rows_at(pos_ref, m, piece_rows)
            k_s[rows, :] = kv_refs[m][:, :width]
            v_s[rows, :] = kv_refs[m][:, width:]
        kt_s[...] = k_s[...].astype(jnp.float32).T.astype(jnp.bfloat16)
        seg_row = seg_ref[...].astype(jnp.float32)
        seg_col = jnp.broadcast_to(seg_row, (width, tokens)).T
        for start in range(0, tokens, width):
            q_seg = seg_row[:, start : start + width]
            key_id = lax.broadcasted_iota(jnp.int32, (tokens, width), 0)
            query_id = start + lax.broadcasted_iota(jnp.int32, (tokens, width), 1)
            allowed = (seg_col == q_seg) & (key_id <= query_id)
            bias_s[:, start : start + width] = jnp.where(allowed, 0.0, MASKED)
        dk_s[...] = jnp.zeros_like(dk_s)
        dv_s[...] = jnp.zeros_like(dv_s)

    for m in range(n):
        g_s[rows_at(pos_ref, m, piece_rows), :] = g_refs[m][...]

    for start in range(0, tokens, block):
        stop = start + block
        c = cos_ref[:, start:stop]
        t = sin_ref[:, start:stop]
        grad_k, grad_v = [], []
        for lane in range(0, g_s.shape[1], width):
            q = q_ref[start:stop, lane : lane + width]
            g = g_s[start:stop, lane : lane + width]
            scores = dot(k_s[:stop, :], q, NT) * to_exponent + bias_s[:stop, start:stop]
            top = jnp.max(scores, 0, keepdims=True)
            shifted = jnp.exp2(scores - top)
            total = jnp.sum(shifted, 0, keepdims=True)
            attention = shifted * (1.0 / total)
            dprobs = dot(v_s[:stop, :], g, NT)
            delta = jnp.sum(attention * dprobs, 0, keepdims=True)
            dscores = (attention * (dprobs - delta)).astype(jnp.bfloat16)
            grad_v.append(dot(attention.astype(jnp.bfloat16), g, NN))
            grad_k.append(dot(dscores, q, NN))
            dq = dot(kt_s[:, :stop], dscores, NN)
            u, w = dq[:half], dq[half:]
            turned = jnp.concatenate([u * c + w * t, w * c - u * t], 0)
            dq_ref[start:stop, lane : lane + width] = turned.T.astype(jnp.bfloat16)
        dv_s[:stop, :] += sum(grad_v[1:], grad_v[0])
        dk_s[:stop, :] += sum(grad_k[1:], grad_k[0])

    @pl.when(head == pl.num_programs(0) - 1)
    def _():
        dk = dk_s[...].T
        c = cos_ref[...]
        t = sin_ref[...]
        u, w = dk[:half], dk[half:]
        turned = jnp.concatenate([u * c + w * t, w * c - u * t], 0)
        dkv_ref[:, :width] = turned.T.astype(jnp.bfloat16)
        dkv_ref[:, width:] = dv_s[...].astype(jnp.bfloat16)


def attention_backward(pos, pieces, queries, segments, cosine, sine):
    n = len(pieces)
    tokens, cols = queries.shape
    width = HEAD_WIDTH
    heads = cols // width
    step = min(HEADS_AT_ONCE, heads) * width
    piece_rows = tokens // n
    bf16, f32 = jnp.bfloat16, jnp.float32
    return pl.pallas_call(
        functools.partial(attention_kernel, n),
        out_shape=[
            jax.ShapeDtypeStruct((tokens, cols), bf16),
            jax.ShapeDtypeStruct((tokens, 2 * width), bf16),
        ],
        grid_spec=pltpu.PrefetchScalarGridSpec(
            num_scalar_prefetch=1,
            grid=(cols // step,),
            in_specs=[pl.BlockSpec((piece_rows, step), lambda h, p: (0, h))] * n
            + [pl.BlockSpec((piece_rows, 2 * width), lambda h, p: (0, cols // (2 * width)))] * n
            + [
                pl.BlockSpec((tokens, step), lambda h, p: (0, h)),
                pl.BlockSpec((1, tokens), lambda h, p: (0, 0)),
                pl.BlockSpec((width // 2, tokens), lambda h, p: (0, 0)),
                pl.BlockSpec((width // 2, tokens), lambda h, p: (0, 0)),
            ],
            out_specs=[
                pl.BlockSpec((tokens, step), lambda h, p: (0, h)),
                pl.BlockSpec((tokens, 2 * width), lambda h, p: (0, 0)),
            ],
            scratch_shapes=[
                pltpu.VMEM((tokens, width), bf16),
                pltpu.VMEM((tokens, width), bf16),
                pltpu.VMEM((width, tokens), bf16),
                pltpu.VMEM((tokens, tokens), f32),
                pltpu.VMEM((tokens, step), bf16),
                pltpu.VMEM((tokens, width), f32),
                pltpu.VMEM((tokens, width), f32),
            ],
        ),
        compiler_params=pltpu.CompilerParams(
            dimension_semantics=("arbitrary",), vmem_limit_bytes=ATTENTION_VMEM
        ),
        cost_estimate=pl.CostEstimate(
            flops=10 * heads * tokens * tokens * width,
            bytes_accessed=6 * tokens * cols,
            transcendentals=heads * tokens * tokens,
        ),
        name="attention_backward",
    )(pos, *pieces, *pieces, queries, segments, cosine, sine)


def weight_copies(weight_ref, weight_s, arrived):
    blocks, block = weight_s.shape[:2]
    copies = [
        pltpu.make_async_copy(
            weight_ref.at[pl.ds(b * block, block), :], weight_s.at[b], arrived.at[b]
        )
        for b in range(blocks)
    ]
    for copy in copies:
        copy.start()
    return copies


def head_columns(pos_ref, source, share, kv_width):
    head = pos_ref[source] // share
    return [
        pl.ds(pl.multiple_of(side * kv_width + head * HEAD_WIDTH, HEAD_WIDTH), HEAD_WIDTH)
        for side in range(2)
    ]


def product_with(pos_ref, sources, share, parts_s, block_ref):
    kv_width = block_ref.shape[1] // 2
    picked = [
        block_ref[:, cols]
        for source in sources
        for cols in head_columns(pos_ref, source, share, kv_width)
    ]
    return dot(parts_s[...], jnp.concatenate(picked, 1), NT)


def first_kernel(n, share, sources, pos_ref, *refs):
    part_refs, weight_ref = refs[: len(sources)], refs[len(sources)]
    out_ref, parts_s, weight_s, arrived = refs[len(sources) + 1 :]
    copies = weight_copies(weight_ref, weight_s, arrived)
    piece_rows = parts_s.shape[0] // n
    wide = part_refs[0].shape[1]
    block = weight_s.shape[1]
    for i, part_ref in enumerate(part_refs):
        for m in range(n):
            rows = slice(m * piece_rows, (m + 1) * piece_rows)
            parts_s[rows, i * wide : (i + 1) * wide] = part_ref[rows_at(pos_ref, m, piece_rows), :]
    for b, copy in enumerate(copies):
        copy.wait()
        out_ref[:, b * block : (b + 1) * block] = product_with(
            pos_ref, sources, share, parts_s, weight_s.at[b]
        )


def input_kernel(n, share, sources, pos_ref, *refs):
    part_refs, weight_ref, first_ref = refs[:n], refs[n], refs[n + 1]
    out_refs, kv_ref = refs[n + 2 : 2 * n + 2], refs[2 * n + 2]
    parts_s, weight_s, arrived, *sums = refs[2 * n + 3 :]
    copies = weight_copies(weight_ref, weight_s, arrived)
    total = sums[0] if share > 1 else kv_ref
    width = HEAD_WIDTH
    kv_width = kv_ref.shape[1] // 2
    piece_rows = out_refs[0].shape[0]
    block = weight_s.shape[1]
    if share > 1:
        total[...] = jnp.zeros_like(total)
    for source in range(n):
        columns = head_columns(pos_ref, source, share, kv_width)
        for m in range(n):
            rows = slice(m * piece_rows, (m + 1) * piece_rows)
            part = part_refs[source][rows_at(pos_ref, m, piece_rows), :]
            if source in sources:
                at = sources.index(source) * 2 * width
                parts_s[rows, at : at + 2 * width] = part
            for side, cols in enumerate(columns):
                own = part[:, side * width : (side + 1) * width]
                if share > 1:
                    total[rows, cols] += own.astype(jnp.float32)
                else:
                    total[rows, cols] = own
    if share > 1:
        kv_ref[...] = total[...].astype(kv_ref.dtype)
    for b, copy in enumerate(copies):
        copy.wait()
        cols = slice(b * block, (b + 1) * block)
        product = product_with(pos_ref, sources, share, parts_s, weight_s.at[b])
        product = (product + first_ref[:, cols]).astype(jnp.bfloat16)
        for m in range(n):
            out_refs[m][:, cols] = product[m * piece_rows : (m + 1) * piece_rows]


def first_products(pos, sources, parts, weight, n, share):
    tokens, wide = parts[0].shape
    rows, cols = weight.shape
    block = min(FEATURE_BLOCK, rows)
    vmem = pl.BlockSpec(memory_space=pltpu.VMEM)
    return pl.pallas_call(
        functools.partial(first_kernel, n, share, sources),
        out_shape=jax.ShapeDtypeStruct((tokens, rows), jnp.float32),
        in_specs=[pl.BlockSpec(memory_space=pltpu.SMEM)]
        + [vmem] * len(parts)
        + [pl.BlockSpec(memory_space=pltpu.HBM)],
        out_specs=vmem,
        scratch_shapes=[
            pltpu.VMEM((tokens, len(parts) * wide), jnp.bfloat16),
            pltpu.VMEM((rows // block, block, cols), jnp.bfloat16),
            pltpu.SemaphoreType.DMA((rows // block,)),
        ],
        compiler_params=pltpu.CompilerParams(vmem_limit_bytes=VMEM_LIMIT),
        cost_estimate=pl.CostEstimate(
            flops=2 * tokens * rows * wide * len(parts),
            bytes_accessed=2 * rows * cols + 4 * tokens * rows,
            transcendentals=0,
        ),
        name="first_products",
    )(pos, *parts, pltpu.with_memory_space_constraint(weight, pltpu.HBM))


def input_gradient(pos, sources, parts, weight, first, share):
    n = len(parts)
    tokens, wide = parts[0].shape
    rows, cols = weight.shape
    bf16 = jnp.bfloat16
    block = min(FEATURE_BLOCK, rows)
    vmem = pl.BlockSpec(memory_space=pltpu.VMEM)
    out = pl.pallas_call(
        functools.partial(input_kernel, n, share, sources),
        out_shape=[jax.ShapeDtypeStruct((tokens // n, rows), bf16)] * n
        + [jax.ShapeDtypeStruct((tokens, cols), bf16)],
        in_specs=[pl.BlockSpec(memory_space=pltpu.SMEM)]
        + [vmem] * n
        + [pl.BlockSpec(memory_space=pltpu.HBM), vmem],
        out_specs=[vmem] * (n + 1),
        scratch_shapes=[
            pltpu.VMEM((tokens, len(sources) * wide), bf16),
            pltpu.VMEM((rows // block, block, cols), bf16),
            pltpu.SemaphoreType.DMA((rows // block,)),
        ]
        + ([pltpu.VMEM((tokens, cols), jnp.float32)] if share > 1 else []),
        compiler_params=pltpu.CompilerParams(vmem_limit_bytes=VMEM_LIMIT),
        cost_estimate=pl.CostEstimate(
            flops=2 * tokens * rows * wide * len(sources),
            bytes_accessed=2 * (2 * tokens * cols + rows * cols + 3 * tokens * rows),
            transcendentals=0,
        ),
        name="input_gradient",
    )(pos, *parts, pltpu.with_memory_space_constraint(weight, pltpu.HBM), first)
    return out[:n], out[n]


def weight_kernel(n, halves, pos_ref, *refs):
    x_refs, kv_ref = refs[:n], refs[n]
    out_refs, x_s = refs[n + 1 : -1], refs[-1]
    piece_rows = x_refs[0].shape[0]
    for m in range(n):
        x_s[m * piece_rows : (m + 1) * piece_rows, :] = x_refs[m][...]
    if halves:
        cols = kv_ref.shape[1] // 2
        mine = pos_ref[n]
        for out_ref, side in zip(out_refs, (1 - mine, mine)):
            picked = kv_ref[:, pl.ds(pl.multiple_of(side * cols, cols), cols)]
            out_ref[...] = dot(x_s[...], picked, TN).astype(out_ref.dtype)
    else:
        out_refs[0][...] = dot(x_s[...], kv_ref[...], TN)


def weight_gradient(pos, pieces, kv_grad, halves):
    n = len(pieces)
    rows = pieces[0].shape[1]
    tokens, cols = kv_grad.shape
    vmem = pl.BlockSpec(memory_space=pltpu.VMEM)
    if halves:
        out_shape = [
            jax.ShapeDtypeStruct((rows, cols // 2), jnp.bfloat16),
            jax.ShapeDtypeStruct((rows, cols // 2), jnp.float32),
        ]
    else:
        out_shape = [jax.ShapeDtypeStruct((rows, cols), jnp.float32)]
    return pl.pallas_call(
        functools.partial(weight_kernel, n, halves),
        out_shape=out_shape,
        in_specs=[pl.BlockSpec(memory_space=pltpu.SMEM)] + [vmem] * (n + 1),
        out_specs=[vmem] * len(out_shape),
        scratch_shapes=[pltpu.VMEM((tokens, rows), jnp.bfloat16)],
        compiler_params=pltpu.CompilerParams(vmem_limit_bytes=VMEM_LIMIT),
        cost_estimate=pl.CostEstimate(
            flops=2 * tokens * rows * cols,
            bytes_accessed=2 * tokens * (rows + cols) + 4 * rows * cols,
            transcendentals=0,
        ),
        name="weight_gradient",
    )(pos, *pieces, kv_grad)


def join_kernel(order, relayed, begun, pos_ref, *refs):
    count = len(order)
    cols = refs[0].shape[1]
    out_ref, done = refs[-2:]
    at = [pl.ds(pl.multiple_of(pos_ref[m] * cols, cols), cols) for m in order]
    for i in range(count):
        if i == 0 and relayed:
            taken = pos_ref[pos_ref.shape[0] - 1] == 1

            @pl.when(taken)
            def _():
                pltpu.make_async_copy(refs[count], out_ref.at[:, at[0]], done.at[0]).start()

            @pl.when(jnp.logical_not(taken))
            def _():
                pltpu.make_async_copy(refs[0], out_ref.at[:, at[0]], done.at[0]).start()

        else:
            pltpu.make_async_copy(refs[i], out_ref.at[:, at[i]], done.at[i]).start()
    for i in range(count):
        pltpu.make_async_copy(refs[i], out_ref.at[:, at[i]], done.at[i]).wait()


def join_columns(pos, order, pieces, n, begun=None):
    rows, cols = pieces[0].shape
    vmem = pl.BlockSpec(memory_space=pltpu.VMEM)
    hbm = pl.BlockSpec(memory_space=pltpu.HBM)
    started = begun is not None
    return pl.pallas_call(
        functools.partial(join_kernel, order, len(pieces) > len(order), started),
        out_shape=jax.ShapeDtypeStruct((rows, n * cols), pieces[0].dtype),
        in_specs=[pl.BlockSpec(memory_space=pltpu.SMEM)]
        + [vmem] * len(pieces)
        + ([hbm] if started else []),
        out_specs=hbm,
        scratch_shapes=[pltpu.SemaphoreType.DMA((len(order),))],
        input_output_aliases={1 + len(pieces): 0} if started else {},
        compiler_params=pltpu.CompilerParams(vmem_limit_bytes=VMEM_LIMIT),
        cost_estimate=pl.CostEstimate(
            flops=0, bytes_accessed=4 * rows * len(order) * cols, transcendentals=0
        ),
        name="join_columns",
    )(pos, *pieces, *([begun] if started else []))


def lay_out_kernel(in_ref, out_ref):
    cols = in_ref.shape[2]
    for block in range(in_ref.shape[0]):
        out_ref[:, block * cols : (block + 1) * cols] = in_ref[block]


def lay_out(blocks):
    n, rows, cols = blocks.shape
    vmem = pl.BlockSpec(memory_space=pltpu.VMEM)
    return pl.pallas_call(
        lay_out_kernel,
        out_shape=jax.ShapeDtypeStruct((rows, n * cols), blocks.dtype),
        in_specs=[vmem],
        out_specs=vmem,
        compiler_params=pltpu.CompilerParams(vmem_limit_bytes=VMEM_LIMIT),
        cost_estimate=pl.CostEstimate(
            flops=0, bytes_accessed=4 * rows * n * cols, transcendentals=0
        ),
        name="lay_out",
    )(blocks)


def swapped(value, mask, axis="ctx"):
    size = lax.axis_size(axis)
    return lax.ppermute(value, axis, [(i, i ^ mask) for i in range(size)])


def to_section_before(value, mask):
    sections, size = lax.axis_size("section"), lax.axis_size("ctx")
    pairs = [
        (s * size + i, (s - 1) * size + (i ^ mask)) for s in range(1, sections) for i in range(size)
    ]
    return lax.ppermute(value, ("section", "ctx"), pairs)


def relayed_section_before(value, mask):
    sections, size = lax.axis_size("section"), lax.axis_size("ctx")
    half = sections // 2
    first = [
        (s * size + i, (s - 1) * size + (i if s == half else i ^ mask))
        for s in range(1, sections)
        for i in range(size)
    ]
    second = [((half - 1) * size + i, (half - 1) * size + (i ^ mask)) for i in range(size)]
    value = lax.ppermute(value, ("section", "ctx"), first)
    return value, lax.ppermute(value, ("section", "ctx"), second)


def after(values, others):
    return lax.optimization_barrier((values, others))[0]


def on_device(layer_input, attn_grad, queries, keys, values, kv_weight, segments, positions):
    frequency, mscale = yarn_table(HEAD_WIDTH)
    width = HEAD_WIDTH
    inputs, grads = layer_input[0, 0], attn_grad[0, 0]
    key_rows, value_rows = keys[0, 0], values[0, 0]
    n = lax.axis_size("ctx")
    me = lax.axis_index("ctx")
    data_size = lax.axis_size("dp")
    tokens, cols = queries.shape[2:]
    kv_heads = key_rows.shape[1] // width
    share = n // kv_heads
    masks = list(range(1, n))[::-1]
    block_of = [me ^ m for m in range(n)]
    section = lax.axis_index("section")
    relay = lax.axis_size("section") == 4 and n == 4
    at_relay = section == lax.axis_size("section") // 2 - 1
    pos = jnp.stack([*block_of, lax.axis_index("dp"), at_relay.astype(jnp.int32)])

    def block(array, at, size):
        return lax.dynamic_slice_in_dim(array, at * size, size, 1)

    def outgoing(m):
        head = block_of[m] // share
        return jnp.concatenate(
            [
                block(grads, block_of[m], cols),
                block(key_rows, head, width),
                block(value_rows, head, width),
            ],
            1,
        )

    sent = {m: swapped(outgoing(m), m) for m in masks}
    pieces = [outgoing(0), *(sent[m] for m in range(1, n))]

    angles = frequency[:, None] * positions.astype(jnp.float32)
    score_scale = width ** (-0.5)
    cosine = jnp.cos(angles) * (mscale * score_scale)
    sine = jnp.sin(angles) * (mscale * score_scale)

    features = inputs.shape[1] // n
    x_out = [block(inputs, block_of[m], features) for m in range(n)]
    far, near = n // 2, 1
    middle = [m for m in masks if m not in (far, near)]
    x_held = after(x_out, pieces)
    x_sent = {m: swapped(x_held[m], m) for m in [*middle, far]}
    x_sent[near] = swapped(x_out[near], near)

    dq, dkv = attention_backward(pos, pieces, queries[0, 0], segments, cosine, sine)
    dkv = after(dkv, [x_sent[m] for m in [near, far]])

    parts = {0: dkv}
    bit = far
    while bit:
        for m in sorted(parts):
            held = after(parts[m], x_sent) if m else parts[m]
            parts[m | bit] = swapped(held, bit)
        bit //= 2
    early = [0, far]
    first = first_products(pos, early, [parts[m] for m in early], kv_weight[0], n, share)
    dq = after(dq, parts[far])
    dq = lax.all_to_all(dq.reshape(n, tokens // n, cols), "ctx", 0, 0, tiled=True)
    parts = [parts[m] for m in range(n)]
    x_pieces = [x_out[0], *(x_sent[m] for m in range(1, n))]

    others = [m for m in range(n) if m not in early]
    in_grads, kv_grad = input_gradient(pos, others, parts, kv_weight[0], first, share)
    order = [*masks, 0]
    in_sent = [to_section_before(in_grads[m], m) for m in order[1:]]
    if relay:
        direct, second = relayed_section_before(in_grads[order[0]], order[0])
        in_sent = [direct, *in_sent, second]
    else:
        in_sent = [to_section_before(in_grads[order[0]], order[0]), *in_sent]

    halves = data_size == 2
    if halves:
        away, home = weight_gradient(pos, x_pieces, kv_grad, True)
        weight_grad = (home + swapped(away, 1, "dp").astype(jnp.float32)) / data_size
    else:
        (rows_part,) = weight_gradient(pos, x_pieces, kv_grad, False)
        weight_grad = lax.psum_scatter(rows_part, "dp", scatter_dimension=1, tiled=True) / data_size

    query_grad = lay_out(dq)
    last = after(pos, (query_grad, weight_grad))
    split = n - 2
    begun = join_columns(last, order[split:], in_sent[split:n], n)
    grad_prev = join_columns(last, order[:split], in_sent[:split] + in_sent[n:], n, begun)
    return (grad_prev[None, None], query_grad[None, None], weight_grad[None])


def solution(mesh):
    return jax.shard_map(
        on_device,
        mesh=mesh,
        in_specs=(
            P("section", "dp", "ctx", None),
            P("section", "dp", "ctx", None),
            P("section", "dp", None, "ctx"),
            P("section", "dp", "ctx", None),
            P("section", "dp", "ctx", None),
            P("section", "ctx", None),
            P("dp", None),
            P("dp", None),
        ),
        out_specs=(
            P("section", "dp", "ctx", None),
            P("section", "dp", "ctx", None),
            P("section", "ctx", "dp"),
        ),
        check_vma=False,
    )
```
